32 devices in a mesh: row: 8 (over y, x, core), col: 4 (over z).
Axes of the slice: x: 2, y: 2, z: 4, core: 2. Of those that a mesh axis runs over, the one named last changes fastest.
Arguments:
- matrix: float32 [9216, 9216], P('row', 'col'), as said below
Outputs:
- factored: float32 [9216, 9216], P('row', 'col')
Inputs may be any that keep to these rules, and one draw needn't show every extreme that they name: `matrix`: Off-diagonal entries are of order one; each diagonal entry lies between 4 * sqrt(256) and 8 * sqrt(256) times that.
All inputs are finite; a program needn't handle non-finite values.
Results may differ from the reference program's by a relative error of at most 0.0001.
Values sent between devices are 32-bit elements; how exact they have to be, the bound alone decides.
No kernel may reach another device: no remote copies, remote signals or barrier semaphores. Data moves between devices by JAX's collectives and lax.ppermute only.
A program may use at most 128 MiB of HBM per device.

```python
import jax
import jax.numpy as jnp
from jax import lax

N = 9216
B = 256
STEPS = 2


def draw_matrix(key, part):
    key_off, key_diag = jax.random.split(key)
    offdiag = jax.random.normal(key_off, (N, N), jnp.float32)
    scale = 4.0 * jnp.sqrt(jnp.float32(B))
    diagonal = scale * jax.random.uniform(key_diag, (N,), jnp.float32, 1.0, 2.0)
    indices = jnp.arange(N, dtype=jnp.int32)
    return jnp.where(indices[:, None] == indices[None, :], diagonal[:, None], offdiag)


def setup_inputs(seed: int = 0) -> dict:
    streams_of = jax.random.split(jax.random.key(seed), 2)
    matrix = draw_matrix(jax.random.fold_in(streams_of[1], 71), 0)
    return {"matrix": matrix}


def mult(left, right):
    return jnp.dot(left, right, precision=lax.Precision.HIGHEST, preferred_element_type=jnp.float32)


def reference(matrix):
    work = matrix
    row_ids = jnp.arange(N, dtype=jnp.int32)[:, None]
    col_ids = jnp.arange(N, dtype=jnp.int32)[None, :]
    eye = jnp.eye(B, dtype=jnp.float32)
    for step in range(STEPS):
        lead = step * B
        block = work[lead:lead + B, lead:lead + B]
        panel = work[:, lead:lead + B]
        upper = work[lead:lead + B, :]
        inverse = 1.0 / jnp.diagonal(block)
        first = inverse[:, None] * (2.0 * eye - block * inverse[None, :])
        second = mult(first, 2.0 * eye - mult(block, first))
        lower = mult(panel, second)
        update = mult(lower, upper)
        picked = jnp.take(lower, jnp.clip(col_ids[0] - lead, 0, B - 1), axis=1)
        below = row_ids >= lead + B
        right = col_ids >= lead + B
        inside = (col_ids >= lead) & (col_ids < lead + B)
        work = jnp.where(below & right, work - update, jnp.where(below & inside, picked, work))
    return work
```

```python
import jax
import jax.numpy as jnp
from jax import lax
from jax.experimental import pallas as pl
from jax.experimental.pallas import tpu as pltpu
from jax.sharding import PartitionSpec as P


B = 256
STEPS = 2
W = STEPS * B


def from_root(array, axis, root):
    mine = lax.axis_index(axis) == root
    return lax.psum(jnp.where(mine, array, jnp.zeros_like(array)), axis)


def mult(left, right):
    return jnp.dot(left, right, precision=lax.Precision.HIGHEST, preferred_element_type=jnp.float32)


def spans(lead, width, extent):
    result = []
    for owner in range(lead // extent, (lead + width - 1) // extent + 1):
        low = max(lead, owner * extent) - owner * extent
        high = min(lead + width, (owner + 1) * extent) - owner * extent
        result.append((owner, low, high))
    return result


def joined_from(array, axis, lead, extent, dim):
    pieces = [
        from_root(lax.slice_in_dim(array, low, high, axis=dim), axis, owner)
        for owner, low, high in spans(lead, B, extent)
    ]
    return jnp.concatenate(pieces, axis=dim)


def inverse_of(block, eye):
    inverse = 1.0 / jnp.diagonal(block)
    first = inverse[:, None] * (2.0 * eye - block * inverse[None, :])
    return mult(first, 2.0 * eye - mult(block, first))


def general(tile):
    rows, cols = tile.shape
    row_ids = lax.axis_index("row") * rows + jnp.arange(rows, dtype=jnp.int32)[:, None]
    col_ids = lax.axis_index("col") * cols + jnp.arange(cols, dtype=jnp.int32)[None, :]
    eye = jnp.eye(B, dtype=jnp.float32)
    for step in range(STEPS):
        lead = step * B
        panel = joined_from(tile, "col", lead, cols, 1)
        joined = joined_from(jnp.concatenate([tile, panel], axis=1), "row", lead, rows, 0)
        upper = joined[:, :cols]
        lower = mult(panel, inverse_of(joined[:, cols:], eye))
        update = mult(lower, upper)
        picked = jnp.take(lower, jnp.clip(col_ids[0] - lead, 0, B - 1), axis=1)
        below = row_ids >= lead + B
        right = col_ids >= lead + B
        inside = (col_ids >= lead) & (col_ids < lead + B)
        tile = jnp.where(below & right, tile - update, jnp.where(below & inside, picked, tile))
    return tile


ANY = pl.BlockSpec(memory_space=pl.ANY)
SM = pl.BlockSpec(memory_space=pltpu.SMEM)
VM = pl.BlockSpec(memory_space=pltpu.VMEM)
F32 = jnp.float32
BF16 = jnp.bfloat16


def split(x):
    hi = x.astype(BF16)
    return hi, (x - hi.astype(F32)).astype(BF16)


def dot(a, b):
    return jnp.dot(a, b, preferred_element_type=F32)


def dot3(a, b):
    (ahi, alo), (bhi, blo) = a, b
    return dot(jnp.concatenate([ahi, ahi, alo], 1), jnp.concatenate([bhi, blo, bhi], 0))


def hdot(a, b):
    return jnp.dot(a, b, precision=lax.Precision.HIGHEST, preferred_element_type=F32)


def among(value, members):
    cond = value == members[0]
    for member in members[1:]:
        cond = cond | (value == member)
    return cond


def onchip(shape, dtype=F32):
    return pltpu.VMEM(shape, dtype)


def choose(ids, sources, shapes, cases):
    def body(ids, *refs):
        outs = refs[len(sources):len(sources) + len(shapes)]
        sem = refs[-1]
        for rs, zs, moves in cases:
            cond = None
            if rs is not None:
                cond = among(ids[0], rs)
            if zs is not None:
                other = among(ids[1], zs)
                cond = other if cond is None else cond & other

            @pl.when(cond)
            def _(moves=moves):
                copies = [
                    pltpu.make_async_copy(refs[s].at[view], outs[o].at[to], sem.at[k])
                    for k, (s, view, o, to) in enumerate(moves)
                ]
                for copy in copies:
                    copy.start()
                for copy in copies:
                    copy.wait()

    most = max(len(moves) for _, _, moves in cases)
    return pl.pallas_call(
        body,
        out_shape=tuple(onchip(s) for s in shapes),
        in_specs=[SM] + [ANY] * len(sources),
        out_specs=(VM,) * len(shapes),
        scratch_shapes=[pltpu.SemaphoreType.DMA((most,))],
        compiler_params=pltpu.CompilerParams(vmem_limit_bytes=1 * 2**20),
    )(ids, *sources)


def factors(ids, dcore, dmate):
    def body(ids, dcore, dmate, w_ref, l_ref, d, sem):
        for odd, ref in ((0, dcore), (1, dmate)):

            @pl.when(ids[0] % 2 == odd)
            def _(ref=ref):
                copy = pltpu.make_async_copy(ref, d, sem)
                copy.start()
                copy.wait()

        blk = lambda i, j: d[i * B:(i + 1) * B, j * B:(j + 1) * B]
        eye = (
            lax.broadcasted_iota(jnp.int32, (B, B), 0)
            == lax.broadcasted_iota(jnp.int32, (B, B), 1)
        )

        def second(block):
            diag = jnp.where(eye, block, 0.0)
            down = 1.0 / jnp.sum(diag, axis=1, keepdims=True)
            across = 1.0 / jnp.sum(diag, axis=0, keepdims=True)
            two = jnp.where(eye, 2.0, 0.0)
            first = down * (two - block * across)
            return hdot(first, two - hdot(block, first))

        s0 = second(blk(0, 0))
        upper = blk(0, 1)
        l10 = hdot(blk(1, 0), s0)
        s1 = second(blk(1, 1) - hdot(l10, upper))
        w_ref[:B, :B] = s0
        w_ref[B:, B:] = s1
        w_ref[:B, B:] = -hdot(s0, hdot(upper, s1))
        w_ref[B:, :B] = jnp.zeros((B, B), F32)
        l_ref[...] = l10

    return pl.pallas_call(
        body,
        out_shape=(onchip((W, W)), onchip((B, B))),
        in_specs=[SM, ANY, ANY],
        out_specs=(VM, VM),
        scratch_shapes=[pltpu.VMEM((W, W), F32), pltpu.SemaphoreType.DMA],
        compiler_params=pltpu.CompilerParams(vmem_limit_bytes=8 * 2**20),
        name="factors",
    )(ids, dcore, dmate)


def upper_split(ids, tile, parts):
    cols = tile.shape[1]
    h = W // 4
    table = {
        1: (1, 0, 1, 1),
        2: (2, 13, 3, 4),
        3: (5, 12, 6, 7),
        4: (12, 5, 7, 6),
        5: (13, 2, 4, 3),
        6: (8, 10, 9, 11),
        7: (10, 8, 11, 9),
    }

    def body(ids, tile, *refs):
        parts, (out, buf, sem) = refs[:14], refs[14:]
        r = ids[0]

        @pl.when(r == 0)
        def _():
            for q in range(4):
                pltpu.make_async_copy(
                    tile.at[q * h:(q + 1) * h], buf.at[q], sem.at[q]
                ).start()

        for row, picks in table.items():

            @pl.when(r == row)
            def _(picks=picks):
                for q, k in enumerate(picks):
                    view = parts[k]
                    if k == 1:
                        at = (0, 0, h, 2 * h)[q]
                        view = view.at[at:at + h]
                    pltpu.make_async_copy(view, buf.at[q], sem.at[q]).start()

        for q in range(4):
            pltpu.make_async_copy(tile.at[:h], buf.at[q], sem.at[q]).wait()
            hi, lo = split(buf[q])
            out[q * h:(q + 1) * h] = hi
            out[W + q * h:W + (q + 1) * h] = lo

    return pl.pallas_call(
        body,
        out_shape=onchip((2 * W, cols), BF16),
        in_specs=[SM, ANY] + [ANY] * 14,
        out_specs=VM,
        scratch_shapes=[pltpu.VMEM((4, h, cols), F32), pltpu.SemaphoreType.DMA((4,))],
        compiler_params=pltpu.CompilerParams(vmem_limit_bytes=10 * 2**20),
        name="upper_split",
    )(ids, tile, *parts)


def update_call(ids, tile, lo, hi, sources, wmat, l10, u2, prev):
    rows, cols = tile.shape
    n = hi - lo
    rb = max(d for d in range(16, 385, 16) if n % d == 0)
    count = n // rb
    arrays = [x for item in sources for x in item]
    fast = pltpu.with_memory_space_constraint(tile, pltpu.VMEM)

    def body(*refs):
        ids, tile, wm, l10, u2 = refs[:5]
        parts = refs[5:5 + len(arrays)]
        rest = refs[5 + len(arrays):]
        if prev is not None:
            rest = rest[1:]
        out, pbuf, obuf, psem, osem = rest
        r, z = ids[0], ids[1]
        for place in range(1, 4):

            @pl.when(z == place)
            def _(place=place):
                at = 0
                copies = []
                for k in range(len(sources)):
                    ref = parts[3 * k + place - 1]
                    size = ref.shape[0]
                    copies.append(
                        pltpu.make_async_copy(ref, pbuf.at[at:at + size], psem.at[k])
                    )
                    at += size
                for copy in copies:
                    copy.start()
                for copy in copies:
                    copy.wait()

        @pl.when(z == 0)
        def _():
            pbuf[...] = tile[lo:hi, :W]

        ws = split(wm[...])
        ts = split(l10[...])

        def put(i):
            at = pl.multiple_of(i * rb, rb)
            return pltpu.make_async_copy(
                obuf.at[pl.ds(at, rb)], out.at[pl.ds(lo + at, rb)], osem.at[i]
            )

        def block(i, carry):
            at = pl.multiple_of(i * rb, rb)
            span = pl.ds(at, rb)
            ids_of = r * rows + lo + at + lax.broadcasted_iota(jnp.int32, (rb, 1), 0)
            ps = split(pbuf[span])
            l0 = dot3([x[:, :B] for x in ps], [x[:B, :B] for x in ws])
            l1 = dot3(ps, [x[:, B:] for x in ws])
            l1s = split(jnp.where(ids_of >= W, l1, 0.0))
            l0s = split(jnp.where(ids_of >= B, l0, 0.0) - dot3(l1s, ts))
            top = jnp.concatenate([l0s[0], l1s[0]], 1)
            low = jnp.concatenate([l0s[1], l1s[1]], 1)
            both = jnp.concatenate([top, top], 1)
            for j in range(cols // B):
                part = slice(j * B, (j + 1) * B)
                acc = dot(low, u2[:W, part]) + dot(both, u2[:, part])
                new = tile[pl.ds(lo + at, rb), part] - acc
                if j < STEPS:
                    lower = l0 if j == 0 else l1
                    new = jnp.where((z == 0) & (ids_of >= (j + 1) * B), lower, new)
                obuf[span, part] = new
            put(i).start()
            return carry

        lax.fori_loop(0, count, block, 0)

        def finish(i, carry):
            put(i).wait()
            return carry

        lax.fori_loop(0, count, finish, 0)

    operands = [ids, fast, wmat, l10, u2] + arrays
    specs = [SM, VM, VM, VM, VM] + [ANY] * len(arrays)
    aliases = {}
    if prev is not None:
        aliases = {len(operands): 0}
        operands.append(prev)
        specs.append(ANY)
    return pl.pallas_call(
        body,
        out_shape=jax.ShapeDtypeStruct(tile.shape, tile.dtype),
        in_specs=specs,
        out_specs=ANY,
        scratch_shapes=[
            pltpu.VMEM((n, W), F32),
            pltpu.VMEM((n, cols), F32),
            pltpu.SemaphoreType.DMA((len(sources),)),
            pltpu.SemaphoreType.DMA((count,)),
        ],
        input_output_aliases=aliases,
        compiler_params=pltpu.CompilerParams(vmem_limit_bytes=26 * 2**20),
    )(*operands)


def ring(tile, across):
    rows, cols = tile.shape
    r = lax.axis_index("row")
    z = lax.axis_index("col")
    ids = jnp.stack([r, z]).astype(jnp.int32)

    def col_move(x, who, source, target):
        pairs = [(q * across + source, q * across + target) for q in who]
        return lax.ppermute(x, ("row", "col"), pairs)

    def row_move(x, pairs):
        return lax.ppermute(x, "row", pairs)

    def pick(*args):
        return choose(ids, *args)

    h = W // 4
    base = pltpu.with_memory_space_constraint(tile, pltpu.HBM)
    full = slice(0, W)
    whole = slice(None)
    qs = lambda i, j=None: slice(i * h, (i + 1 if j is None else j) * h)
    marks = [0, B, W] + [W + -(-(rows - W) * k // (TAIL * 32)) * 32 for k in range(1, TAIL)] + [rows]
    names = ["A1", "A2"] + [f"B{k + 1}" for k in range(TAIL)]
    cuts = dict(zip(names, zip(marks, marks[1:])))
    panels = [(0, (slice(*c), full), k, whole) for k, c in enumerate(cuts.values())]
    n = len(names)
    uppers = [(0, qs(1), n, whole), (0, qs(0), n + 1, qs(0)), (0, qs(2, 4), n + 1, qs(1, 3))]
    others = tuple(range(1, 8))
    *own, q2, q134 = pick(
        [base],
        [(hi - lo, W) for lo, hi in cuts.values()] + [(h, cols), (3 * h, cols)],
        [
            ((0,), (0,), panels + uppers),
            ((0,), (1, 2, 3), uppers),
            (others, (0,), panels),
        ],
    )
    every = tuple(range(8))
    got = {}
    for k, x in zip(cuts, own):
        a = col_move(x, every, 0, 2)
        got[k] = (col_move(a, every, 2, 1), a, col_move(a, every, 2, 3))

    um2 = row_move(q2, [(0, 1)])
    um134 = row_move(q134, [(0, 1)])
    (c1,) = pick(
        [base, um2], [(h, cols)],
        [((0,), None, [(0, qs(0), 0, whole)]), ((1,), None, [(1, whole, 0, whole)])],
    )
    c2, c3 = pick(
        [base, um134], [(h, cols), (h, cols)],
        [
            ((0,), None, [(0, qs(2), 0, whole), (0, qs(3), 1, whole)]),
            ((1,), None, [(1, qs(2), 0, whole), (1, qs(1), 1, whole)]),
        ],
    )
    first, second, third = [(0, 2), (1, 5)], [(2, 6), (5, 7)], [(6, 4), (7, 3)]
    g1 = row_move(c1, first)
    g2 = row_move(c2, first)
    g3 = row_move(c3, first)
    f1 = row_move(g1, second)
    f2 = row_move(g2, second)
    h1 = row_move(f1, third)
    near = [(2, 3), (5, 4)]
    sg1 = row_move(g1, near)
    sg2 = row_move(g2, near)
    sg3 = row_move(g3, near)
    sf1 = row_move(f1, [(6, 7), (7, 6)])
    sf2 = row_move(f2, [(6, 7), (7, 6)])
    sh1 = row_move(h1, [(3, 2), (4, 5)])

    def block_rows(key):
        lo, hi = cuts[key]
        (x,) = pick(
            [base, *got[key]], [(B, W)],
            [((0,), (0,), [(0, (slice(lo, hi), full), 0, whole)])]
            + [((0,), (p,), [(p, whole, 0, whole)]) for p in (1, 2, 3)],
        )
        return x

    d1, d2 = block_rows("A1"), block_rows("A2")
    e1 = row_move(d1, [(0, 2)])
    e2 = row_move(d2, [(0, 4)])
    e3 = row_move(d2, [(0, 2)])
    e4 = row_move(d1, [(0, 4)])
    x1 = row_move(e1, [(2, 6)])
    x2 = row_move(e2, [(4, 6)])
    top, low = slice(0, B), slice(B, W)
    (dcore,) = pick(
        [d1, d2, e1, e2, e3, e4, x1, x2], [(W, W)],
        [
            ((row,), None, [(p, whole, 0, top), (q, whole, 0, low)])
            for row, p, q in ((0, 0, 1), (2, 2, 4), (4, 5, 3), (6, 6, 7))
        ],
    )
    dmate = row_move(dcore, [(i, i + 1) for i in range(0, 8, 2)])

    wmat, l10 = factors(ids, dcore, dmate)
    u2 = upper_split(
        ids, base,
        (um2, um134, g1, g2, g3, sg1, sg2, sg3, f1, f2, sf1, sf2, h1, sh1),
    )
    pieces = [got[k] for k in names]
    late = marks[-2]
    out = update_call(ids, tile, 0, late, pieces[:-1], wmat, l10, u2, None)
    return update_call(ids, tile, late, rows, pieces[-1:], wmat, l10, u2, out)


TAIL = 3


def solution(mesh):
    across = mesh.shape["col"]

    def on_device(tile):
        rows, cols = tile.shape
        fits = rows >= 2 * W and cols >= W and rows % 128 == 0 and cols % B == 0
        if fits and mesh.shape["row"] == 8 and across == 4:
            return ring(tile, across)
        return general(tile)

    return jax.shard_map(
        on_device,
        mesh=mesh,
        in_specs=(P("row", "col"),),
        out_specs=P("row", "col"),
        check_vma=False,
    )
```

```python
import jax
import jax.numpy as jnp
from jax import lax
from jax.experimental import pallas as pl
from jax.experimental.pallas import tpu as pltpu
from jax.sharding import PartitionSpec as P


B = 256
STEPS = 2
W = STEPS * B


def from_root(array, axis, root):
    mine = lax.axis_index(axis) == root
    return lax.psum(jnp.where(mine, array, jnp.zeros_like(array)), axis)


def mult(left, right):
    return jnp.dot(left, right, precision=lax.Precision.HIGHEST, preferred_element_type=jnp.float32)


def spans(lead, width, extent):
    result = []
    for owner in range(lead // extent, (lead + width - 1) // extent + 1):
        low = max(lead, owner * extent) - owner * extent
        high = min(lead + width, (owner + 1) * extent) - owner * extent
        result.append((owner, low, high))
    return result


def joined_from(array, axis, lead, extent, dim):
    pieces = [
        from_root(lax.slice_in_dim(array, low, high, axis=dim), axis, owner)
        for owner, low, high in spans(lead, B, extent)
    ]
    return jnp.concatenate(pieces, axis=dim)


def inverse_of(block, eye):
    inverse = 1.0 / jnp.diagonal(block)
    first = inverse[:, None] * (2.0 * eye - block * inverse[None, :])
    return mult(first, 2.0 * eye - mult(block, first))


def general(tile):
    rows, cols = tile.shape
    row_ids = lax.axis_index("row") * rows + jnp.arange(rows, dtype=jnp.int32)[:, None]
    col_ids = lax.axis_index("col") * cols + jnp.arange(cols, dtype=jnp.int32)[None, :]
    eye = jnp.eye(B, dtype=jnp.float32)
    for step in range(STEPS):
        lead = step * B
        panel = joined_from(tile, "col", lead, cols, 1)
        joined = joined_from(jnp.concatenate([tile, panel], axis=1), "row", lead, rows, 0)
        upper = joined[:, :cols]
        lower = mult(panel, inverse_of(joined[:, cols:], eye))
        update = mult(lower, upper)
        picked = jnp.take(lower, jnp.clip(col_ids[0] - lead, 0, B - 1), axis=1)
        below = row_ids >= lead + B
        right = col_ids >= lead + B
        inside = (col_ids >= lead) & (col_ids < lead + B)
        tile = jnp.where(below & right, tile - update, jnp.where(below & inside, picked, tile))
    return tile


ANY = pl.BlockSpec(memory_space=pl.ANY)
SM = pl.BlockSpec(memory_space=pltpu.SMEM)
VM = pl.BlockSpec(memory_space=pltpu.VMEM)
F32 = jnp.float32
BF16 = jnp.bfloat16


def split(x):
    hi = x.astype(BF16)
    return hi, (x - hi.astype(F32)).astype(BF16)


def dot(a, b):
    return jnp.dot(a, b, preferred_element_type=F32)


def dot3(a, b):
    (ahi, alo), (bhi, blo) = a, b
    return dot(jnp.concatenate([ahi, ahi, alo], 1), jnp.concatenate([bhi, blo, bhi], 0))


def among(value, members):
    cond = value == members[0]
    for member in members[1:]:
        cond = cond | (value == member)
    return cond


def onchip(shape, dtype=F32):
    return pltpu.VMEM(shape, dtype)


def choose(ids, sources, shapes, cases):
    def body(ids, *refs):
        outs = refs[len(sources):len(sources) + len(shapes)]
        sem = refs[-1]
        for rs, zs, moves in cases:
            cond = None
            if rs is not None:
                cond = among(ids[0], rs)
            if zs is not None:
                other = among(ids[1], zs)
                cond = other if cond is None else cond & other

            @pl.when(cond)
            def _(moves=moves):
                copies = [
                    pltpu.make_async_copy(refs[s].at[view], outs[o].at[to], sem.at[k])
                    for k, (s, view, o, to) in enumerate(moves)
                ]
                for copy in copies:
                    copy.start()
                for copy in copies:
                    copy.wait()

    most = max(len(moves) for _, _, moves in cases)
    return pl.pallas_call(
        body,
        out_shape=tuple(onchip(s) for s in shapes),
        in_specs=[SM] + [ANY] * len(sources),
        out_specs=(VM,) * len(shapes),
        scratch_shapes=[pltpu.SemaphoreType.DMA((most,))],
        compiler_params=pltpu.CompilerParams(vmem_limit_bytes=1 * 2**20),
    )(ids, *sources)


def factors(ids, dcore, dmate):
    def body(ids, dcore, dmate, w_ref, l_ref, d, sem):
        for odd, ref in ((0, dcore), (1, dmate)):

            @pl.when(ids[0] % 2 == odd)
            def _(ref=ref):
                copy = pltpu.make_async_copy(ref, d, sem)
                copy.start()
                copy.wait()

        blk = lambda i, j: d[i * B:(i + 1) * B, j * B:(j + 1) * B]
        eye = (
            lax.broadcasted_iota(jnp.int32, (B, B), 0)
            == lax.broadcasted_iota(jnp.int32, (B, B), 1)
        )

        def product(a, b):
            return dot3(split(a), split(b))

        def second(block):
            diag = jnp.where(eye, block, 0.0)
            down = 1.0 / jnp.sum(diag, axis=1, keepdims=True)
            across = 1.0 / jnp.sum(diag, axis=0, keepdims=True)
            two = jnp.where(eye, 2.0, 0.0)
            first = down * (two - block * across)
            return product(first, two - product(block, first))

        s0 = second(blk(0, 0))
        upper = blk(0, 1)
        l10 = product(blk(1, 0), s0)
        s1 = second(blk(1, 1) - product(l10, upper))
        w_ref[:B, :B] = s0
        w_ref[B:, B:] = s1
        w_ref[:B, B:] = -product(s0, product(upper, s1))
        w_ref[B:, :B] = jnp.zeros((B, B), F32)
        l_ref[...] = l10

    return pl.pallas_call(
        body,
        out_shape=(onchip((W, W)), onchip((B, B))),
        in_specs=[SM, ANY, ANY],
        out_specs=(VM, VM),
        scratch_shapes=[pltpu.VMEM((W, W), F32), pltpu.SemaphoreType.DMA],
        compiler_params=pltpu.CompilerParams(vmem_limit_bytes=8 * 2**20),
        name="factors",
    )(ids, dcore, dmate)


def upper_split(ids, tile, parts):
    cols = tile.shape[1]
    h = W // 4
    table = {
        1: (1, 0, 1, 1),
        2: (2, 13, 3, 4),
        3: (5, 12, 6, 7),
        4: (12, 5, 7, 6),
        5: (13, 2, 4, 3),
        6: (8, 10, 9, 11),
        7: (10, 8, 11, 9),
    }

    def body(ids, tile, *refs):
        parts, (out, buf, sem) = refs[:14], refs[14:]
        r = ids[0]

        @pl.when(r == 0)
        def _():
            for q in range(4):
                pltpu.make_async_copy(
                    tile.at[q * h:(q + 1) * h], buf.at[q], sem.at[q]
                ).start()

        for row, picks in table.items():

            @pl.when(r == row)
            def _(picks=picks):
                for q, k in enumerate(picks):
                    view = parts[k]
                    if k == 1:
                        at = (0, 0, h, 2 * h)[q]
                        view = view.at[at:at + h]
                    pltpu.make_async_copy(view, buf.at[q], sem.at[q]).start()

        for q in range(4):
            pltpu.make_async_copy(tile.at[:h], buf.at[q], sem.at[q]).wait()
            hi, lo = split(buf[q])
            out[q * h:(q + 1) * h] = hi
            out[W + q * h:W + (q + 1) * h] = lo

    return pl.pallas_call(
        body,
        out_shape=onchip((2 * W, cols), BF16),
        in_specs=[SM, ANY] + [ANY] * 14,
        out_specs=VM,
        scratch_shapes=[pltpu.VMEM((4, h, cols), F32), pltpu.SemaphoreType.DMA((4,))],
        compiler_params=pltpu.CompilerParams(vmem_limit_bytes=10 * 2**20),
        name="upper_split",
    )(ids, tile, *parts)


def update_call(ids, tile, lo, hi, sources, wmat, l10, u2, prev):
    rows, cols = tile.shape
    n = hi - lo
    rb = max(d for d in range(16, 385, 16) if n % d == 0)
    count = n // rb
    arrays = [x for item in sources for x in item]
    fast = pltpu.with_memory_space_constraint(tile, pltpu.VMEM)

    def body(*refs):
        ids, tile, wm, l10, u2 = refs[:5]
        parts = refs[5:5 + len(arrays)]
        rest = refs[5 + len(arrays):]
        if prev is not None:
            rest = rest[1:]
        out, pbuf, obuf, psem, osem = rest
        r, z = ids[0], ids[1]
        for place in range(1, 4):

            @pl.when(z == place)
            def _(place=place):
                at = 0
                copies = []
                for k in range(len(sources)):
                    ref = parts[3 * k + place - 1]
                    size = ref.shape[0]
                    copies.append(
                        pltpu.make_async_copy(ref, pbuf.at[at:at + size], psem.at[k])
                    )
                    at += size
                for copy in copies:
                    copy.start()
                for copy in copies:
                    copy.wait()

        @pl.when(z == 0)
        def _():
            pbuf[...] = tile[lo:hi, :W]

        ws = split(wm[...])
        ts = split(l10[...])

        def put(i):
            at = pl.multiple_of(i * rb, rb)
            return pltpu.make_async_copy(
                obuf.at[pl.ds(at, rb)], out.at[pl.ds(lo + at, rb)], osem.at[i]
            )

        def block(i, carry):
            at = pl.multiple_of(i * rb, rb)
            span = pl.ds(at, rb)
            ids_of = r * rows + lo + at + lax.broadcasted_iota(jnp.int32, (rb, 1), 0)
            ps = split(pbuf[span])
            l0 = dot3([x[:, :B] for x in ps], [x[:B, :B] for x in ws])
            l1 = dot3(ps, [x[:, B:] for x in ws])
            l1s = split(jnp.where(ids_of >= W, l1, 0.0))
            l0s = split(jnp.where(ids_of >= B, l0, 0.0) - dot3(l1s, ts))
            top = jnp.concatenate([l0s[0], l1s[0]], 1)
            low = jnp.concatenate([l0s[1], l1s[1]], 1)
            both = jnp.concatenate([top, top], 1)
            for j in range(cols // B):
                part = slice(j * B, (j + 1) * B)
                acc = dot(low, u2[:W, part]) + dot(both, u2[:, part])
                new = tile[pl.ds(lo + at, rb), part] - acc
                if j < STEPS:
                    lower = l0 if j == 0 else l1
                    new = jnp.where((z == 0) & (ids_of >= (j + 1) * B), lower, new)
                obuf[span, part] = new
            put(i).start()
            return carry

        lax.fori_loop(0, count, block, 0)

        def finish(i, carry):
            put(i).wait()
            return carry

        lax.fori_loop(0, count, finish, 0)

    operands = [ids, fast, wmat, l10, u2] + arrays
    specs = [SM, VM, VM, VM, VM] + [ANY] * len(arrays)
    aliases = {}
    if prev is not None:
        aliases = {len(operands): 0}
        operands.append(prev)
        specs.append(ANY)
    return pl.pallas_call(
        body,
        out_shape=jax.ShapeDtypeStruct(tile.shape, tile.dtype),
        in_specs=specs,
        out_specs=ANY,
        scratch_shapes=[
            pltpu.VMEM((n, W), F32),
            pltpu.VMEM((n, cols), F32),
            pltpu.SemaphoreType.DMA((len(sources),)),
            pltpu.SemaphoreType.DMA((count,)),
        ],
        input_output_aliases=aliases,
        compiler_params=pltpu.CompilerParams(vmem_limit_bytes=26 * 2**20),
    )(*operands)


def ring(tile, across):
    rows, cols = tile.shape
    r = lax.axis_index("row")
    z = lax.axis_index("col")
    ids = jnp.stack([r, z]).astype(jnp.int32)

    def col_move(x, who, source, target):
        pairs = [(q * across + source, q * across + target) for q in who]
        return lax.ppermute(x, ("row", "col"), pairs)

    def row_move(x, pairs):
        return lax.ppermute(x, "row", pairs)

    def pick(*args):
        return choose(ids, *args)

    h = W // 4
    base = pltpu.with_memory_space_constraint(tile, pltpu.HBM)
    full = slice(0, W)
    whole = slice(None)
    qs = lambda i, j=None: slice(i * h, (i + 1 if j is None else j) * h)
    marks = [0, B, W] + [W + -(-(rows - W) * k // (TAIL * 32)) * 32 for k in range(1, TAIL)] + [rows]
    names = ["A1", "A2"] + [f"B{k + 1}" for k in range(TAIL)]
    cuts = dict(zip(names, zip(marks, marks[1:])))
    panels = [(0, (slice(*c), full), k, whole) for k, c in enumerate(cuts.values())]
    n = len(names)
    uppers = [(0, qs(1), n, whole), (0, qs(0), n + 1, qs(0)), (0, qs(2, 4), n + 1, qs(1, 3))]
    others = tuple(range(1, 8))
    *own, q2, q134 = pick(
        [base],
        [(hi - lo, W) for lo, hi in cuts.values()] + [(h, cols), (3 * h, cols)],
        [
            ((0,), (0,), panels + uppers),
            ((0,), (1, 2, 3), uppers),
            (others, (0,), panels),
        ],
    )
    every = tuple(range(8))
    got = {}
    for k, x in zip(cuts, own):
        a = col_move(x, every, 0, 2)
        got[k] = (col_move(a, every, 2, 1), a, col_move(a, every, 2, 3))

    um2 = row_move(q2, [(0, 1)])
    um134 = row_move(q134, [(0, 1)])
    (c1,) = pick(
        [base, um2], [(h, cols)],
        [((0,), None, [(0, qs(0), 0, whole)]), ((1,), None, [(1, whole, 0, whole)])],
    )
    c2, c3 = pick(
        [base, um134], [(h, cols), (h, cols)],
        [
            ((0,), None, [(0, qs(2), 0, whole), (0, qs(3), 1, whole)]),
            ((1,), None, [(1, qs(2), 0, whole), (1, qs(1), 1, whole)]),
        ],
    )
    first, second, third = [(0, 2), (1, 5)], [(2, 6), (5, 7)], [(6, 4), (7, 3)]
    g1 = row_move(c1, first)
    g2 = row_move(c2, first)
    g3 = row_move(c3, first)
    f1 = row_move(g1, second)
    f2 = row_move(g2, second)
    h1 = row_move(f1, third)
    near = [(2, 3), (5, 4)]
    sg1 = row_move(g1, near)
    sg2 = row_move(g2, near)
    sg3 = row_move(g3, near)
    sf1 = row_move(f1, [(6, 7), (7, 6)])
    sf2 = row_move(f2, [(6, 7), (7, 6)])
    sh1 = row_move(h1, [(3, 2), (4, 5)])

    def block_rows(key):
        lo, hi = cuts[key]
        (x,) = pick(
            [base, *got[key]], [(B, W)],
            [((0,), (0,), [(0, (slice(lo, hi), full), 0, whole)])]
            + [((0,), (p,), [(p, whole, 0, whole)]) for p in (1, 2, 3)],
        )
        return x

    d1, d2 = block_rows("A1"), block_rows("A2")
    e1 = row_move(d1, [(0, 2)])
    e2 = row_move(d2, [(0, 4)])
    e3 = row_move(d2, [(0, 2)])
    e4 = row_move(d1, [(0, 4)])
    x1 = row_move(e1, [(2, 6)])
    x2 = row_move(e2, [(4, 6)])
    top, low = slice(0, B), slice(B, W)
    (dcore,) = pick(
        [d1, d2, e1, e2, e3, e4, x1, x2], [(W, W)],
        [
            ((row,), None, [(p, whole, 0, top), (q, whole, 0, low)])
            for row, p, q in ((0, 0, 1), (2, 2, 4), (4, 5, 3), (6, 6, 7))
        ],
    )
    dmate = row_move(dcore, [(i, i + 1) for i in range(0, 8, 2)])

    wmat, l10 = factors(ids, dcore, dmate)
    u2 = upper_split(
        ids, base,
        (um2, um134, g1, g2, g3, sg1, sg2, sg3, f1, f2, sf1, sf2, h1, sh1),
    )
    pieces = [got[k] for k in names]
    return update_call(ids, tile, 0, rows, pieces, wmat, l10, u2, None)


TAIL = 3


def solution(mesh):
    across = mesh.shape["col"]

    def on_device(tile):
        rows, cols = tile.shape
        fits = rows >= 2 * W and cols >= W and rows % 128 == 0 and cols % B == 0
        if fits and mesh.shape["row"] == 8 and across == 4:
            return ring(tile, across)
        return general(tile)

    return jax.shard_map(
        on_device,
        mesh=mesh,
        in_specs=(P("row", "col"),),
        out_specs=P("row", "col"),
        check_vma=False,
    )
```
